32 devices in a mesh: dp: 2 (over y), seq: 16 (over z, x, core).
Axes of the slice: x: 2, y: 2, z: 4, core: 2. Of those that a mesh axis runs over, the one named last changes fastest.
Arguments:
- frame_in: bfloat16 [2, 2304, 1024], P('dp', 'seq'), may hold values from -120 to 120
- token_ids: int32 [2, 16, 60], P('dp', 'seq'), may hold values from 0 to 1663
- durations: int32 [2, 16, 60], P('dp', 'seq'), may hold values from 1 to 4, 144 in all within a row
- valid_len: int32 [2], P('dp'), may hold values from 576 to 2304, as said below
- t_bin: int32 [2], P('dp'), may hold values from 0 to 63
- token_table: bfloat16 [1664, 512], P('seq'), may hold values from -6 to 6
- enc_weight: bfloat16 [512, 1024], replicated, may hold values from -0.25 to 0.25
- mod_table: float32 [64, 2048], replicated, may hold values from -1.2 to 2.5
- w_query: bfloat16 [1024, 512], P('seq'), may hold values from -0.1875 to 0.1875
- w_key: bfloat16 [1024, 512], P('seq'), may hold values from -0.1875 to 0.1875
- w_value: bfloat16 [1024, 512], P('seq'), may hold values from -0.1875 to 0.1875
- attn_grad: bfloat16 [2, 2304, 512], P('dp', 'seq'), may hold values from -6 to 6
Outputs:
- attn_out: bfloat16 [2, 2304, 512], P('dp', 'seq')
- frame_grad: bfloat16 [2, 2304, 1024], P('dp', 'seq')
- query_weight_grad: float32 [1024, 512], P('seq')
- key_weight_grad: float32 [1024, 512], P('seq')
- value_weight_grad: float32 [1024, 512], P('seq')
The draws below stay inside these ranges and needn't reach their ends.
Inputs may be any that keep to these rules, and one draw needn't show every extreme that they name: In every slab the 60 durations sum to 144, so each token's frames lie in its own slab; some token lasts 4 frames. `valid_len`: some recording is valid over all 2304 frames.
All inputs are finite; a program needn't handle non-finite values.
Results may differ from the reference program's by a relative error of at most 0.017.
The reference program's roundings to bfloat16 on the way count: a program that leaves them out, or rounds other values in their place, can miss the bound.
Values may be sent and summed in bfloat16 or wider, within the bound.
No kernel may reach another device: no remote copies, remote signals or barrier semaphores. Data moves between devices by JAX's collectives and lax.ppermute only.
A program may use at most 64 MiB of HBM per device.

```python
import math
import jax
import jax.numpy as jnp
import numpy as np
from jax import lax

D = 1024
ENC = 512
HEADS = 8
HD = 64
BLK = 48
NBINS = 64
F_DEV = 144
TOK_DEV = 60
RECS = 2
FRAMES = 2304
VOCAB = 1664
QW = 512
N_SEQ = 16


def draw_frame_in(key, part):
    key_base, key_rows, key_cols = jax.random.split(key, 3)
    row_scale = jnp.exp(jax.random.uniform(key_rows, (RECS, FRAMES, 1), jnp.float32, 0.0, math.log(10.0)))
    col_scale = jnp.exp(jax.random.uniform(key_cols, (1, 1, D), jnp.float32, 0.0, math.log(10.0)))
    base_vals = jnp.clip(jax.random.normal(key_base, (RECS, FRAMES, D), jnp.float32), -4.0, 4.0)
    return (0.3 * base_vals * row_scale * col_scale).astype(jnp.bfloat16)


def draw_valid_len(key, part):
    key_len, key_full = jax.random.split(jax.random.fold_in(key, 17), 2)
    lengths = jax.random.randint(key_len, (RECS,), FRAMES // 4, FRAMES + 1)
    full_rec = jax.random.randint(key_full, (), 0, RECS)
    rec_index = jnp.arange(RECS, dtype=jnp.int32)
    return jnp.where(rec_index == full_rec, FRAMES, lengths).astype(jnp.int32)


def draw_mod_table(key, part):
    key_shift, key_gain = jax.random.split(key, 2)
    shift_vals = 0.3 * jnp.clip(jax.random.normal(key_shift, (NBINS, D), jnp.float32), -4.0, 4.0)
    gain_vals = 0.3 * jnp.clip(jax.random.normal(key_gain, (NBINS, D), jnp.float32), -3.0, 3.0)
    return jnp.concatenate([gain_vals, shift_vals], axis=1)


def place_ends(values, rng, smallest, top_value):
    extent = values.shape
    spot = [jax.random.randint(jax.random.fold_in(rng, axis), (), 0, extent[axis]) for axis in range(len(extent))]
    values = values.at[tuple(spot)].set(smallest)
    longest = extent.index(max(extent))
    spot[longest] = (spot[longest] + 1) % extent[longest]
    return values.at[tuple(spot)].set(top_value)


def level_of(key, dims, cuts, least, largest):
    gain, own = 1.0, jax.random.fold_in(key, 6)
    for dim, blocks in cuts:
        draws = jnp.exp(jax.random.uniform(jax.random.fold_in(own, dim), (blocks,), jnp.float32, least / len(cuts), largest / len(cuts)))
        gain = gain * jnp.repeat(draws, dims[dim] // blocks).reshape([-1 if axis == dim else 1 for axis in range(len(dims))])
    return gain


def rank_table(number_of, lean):
    portions = [(1 << 20) // math.isqrt(standing ** lean) + 1 for standing in range(1, number_of + 1)]
    deviation = 1 + sum(portions) // (1 << 30)
    return np.cumsum(np.array([max(1, weight // deviation) for weight in portions]))


def ranked_ids(own_key, dims, amount, skew):
    grid = rank_table(amount, skew)
    ticket = jax.random.randint(jax.random.fold_in(own_key, 1), dims, 0, int(grid[amount - 1]))
    grade = jnp.searchsorted(jnp.asarray(grid, jnp.int32), ticket, side="right")
    return jax.random.permutation(jax.random.fold_in(own_key, 2), amount)[grade].astype(jnp.int32)


def length_profile(number_of, total, bound, lean):
    weights = [(1 << 20) // math.isqrt(grade ** lean) + 1 for grade in range(2, number_of + 1)]
    surplus, counts = total - bound - (number_of - 1), [1] * (number_of - 1)
    while surplus > 0:
        movable = [i for i in range(number_of - 1) if counts[i] < bound]
        mass, remaining = sum([weights[i] for i in movable]), surplus
        for i in movable:
            addition = min(bound - counts[i], max(1, remaining * weights[i] // mass), surplus)
            counts[i] = counts[i] + addition
            surplus = surplus - addition
    return np.array([bound] + counts)


def ragged_sizes(own_key, count, total, most, slope):
    if count == 2:
        one = jax.random.randint(own_key, (), max(1, total - most), min(most, total - 1) + 1)
        return jnp.stack([one, total - one])
    sizes = jnp.asarray(length_profile(count, total, most, slope), jnp.int32)
    couples = (count - 1) // 2
    donor, receiver = sizes[1:1 + 2 * couples:2], sizes[2:2 + 2 * couples:2]
    slack = jnp.minimum(donor - 1, most - receiver)
    shifted = jax.random.randint(jax.random.fold_in(own_key, 1), (couples,), 0, 1 << 20) % (slack + 1)
    sizes = sizes.at[1:1 + 2 * couples:2].set(donor - shifted).at[2:2 + 2 * couples:2].set(receiver + shifted)
    return sizes[jax.random.permutation(jax.random.fold_in(own_key, 2), count)]


def centred(rng, extent, deviation, most, cuts=(), kind=jnp.bfloat16):
    array = jax.random.normal(rng, extent, jnp.float32) * deviation
    if len(cuts) > 0:
        array = level_of(rng, extent, cuts, -0.22, 0.18) * array
    return jnp.clip(array, min=-most, max=most).astype(kind)


def setup_inputs(seed: int = 0) -> dict:
    key_list = jax.random.split(jax.random.key(seed), 13)
    return {
        "frame_in": draw_frame_in(jax.random.fold_in(key_list[12], 71), 0),
        "token_ids": place_ends(ranked_ids(key_list[1], (RECS, N_SEQ, TOK_DEV), VOCAB, 2), jax.random.fold_in(key_list[1], 3), 0, VOCAB - 1).astype(jnp.int32),
        "durations": jax.vmap(lambda own: ragged_sizes(own, TOK_DEV, F_DEV, 4, 1))(jax.random.split(key_list[2], RECS * N_SEQ)).reshape((RECS, N_SEQ, TOK_DEV)).astype(jnp.int32),
        "valid_len": draw_valid_len(jax.random.fold_in(key_list[12], 71), 0),
        "t_bin": jax.random.randint(key_list[4], (RECS,), 0, NBINS).astype(jnp.int32),
        "token_table": centred(key_list[5], (VOCAB, ENC), 1.0, 6.0, ((0, 16),)),
        "enc_weight": centred(key_list[6], (ENC, D), ENC ** -0.5, 0.25),
        "mod_table": draw_mod_table(jax.random.fold_in(key_list[12], 71), 0),
        "w_query": centred(key_list[8], (D, QW), D ** -0.5, 0.1875, ((0, 16),)),
        "w_key": centred(key_list[9], (D, QW), D ** -0.5, 0.1875, ((0, 16),)),
        "w_value": centred(key_list[10], (D, QW), D ** -0.5, 0.1875, ((0, 16),)),
        "attn_grad": centred(key_list[11], (RECS, FRAMES, QW), 1.0, 6.0, ((0, 2), (1, 16))),
    }


def rounded(values):
    return lax.optimization_barrier(values.astype(jnp.bfloat16))

def attend_window(q_blocks, key_ext, value_ext, grad_out, query_pos, key_pos, valid_end, frames_total):
    n_blocks = q_blocks.shape[0]
    block_len = q_blocks.shape[1]
    key_win = jnp.concatenate([key_ext[offset:offset + n_blocks] for offset in range(4)], axis=1).astype(jnp.float32)
    value_win = jnp.concatenate([value_ext[offset:offset + n_blocks] for offset in range(4)], axis=1).astype(jnp.float32)
    q_float = q_blocks.astype(jnp.float32)
    grad_float = grad_out.astype(jnp.float32)
    key_here = key_pos[:, None, :]
    allowed = (key_here >= 0) & (key_here < frames_total) & ((key_here < valid_end) | (query_pos[:, :, None] >= valid_end))
    row_mask = allowed[:, None]
    inv_scale = 1.0 / math.sqrt(q_blocks.shape[-1])
    scores = jnp.einsum('bqhd,bkhd->bhqk', q_float, key_win) * inv_scale
    scores = jnp.where(row_mask, scores, -1e+30)
    row_top = lax.optimization_barrier(jnp.max(scores, axis=-1, keepdims=True))
    shifted_exp = jnp.where(row_mask, jnp.exp(scores - row_top), 0.0)
    attn_prob = shifted_exp / lax.optimization_barrier(jnp.sum(shifted_exp, axis=-1, keepdims=True))
    probs_low = rounded(attn_prob).astype(jnp.float32)
    mixed_out = jnp.einsum('bhqk,bkhd->bqhd', probs_low, value_win).astype(jnp.bfloat16)
    grad_probs = jnp.einsum('bqhd,bkhd->bhqk', grad_float, value_win)
    centre = lax.optimization_barrier(jnp.sum(attn_prob * grad_probs, axis=-1, keepdims=True))
    grad_scores = rounded(attn_prob * (grad_probs - centre) * inv_scale).astype(jnp.float32)
    grad_query = rounded(jnp.einsum('bhqk,bkhd->bqhd', grad_scores, key_win))
    key_terms = jnp.einsum('bhqk,bqhd->bkhd', grad_scores, q_float)
    value_terms = jnp.einsum('bhqk,bqhd->bkhd', probs_low, grad_float)
    win_terms = jnp.concatenate([key_terms, value_terms], axis=2)
    pieces = win_terms.reshape(n_blocks, 4, block_len, win_terms.shape[2], win_terms.shape[3])
    folded = jnp.zeros((n_blocks + 3,) + pieces.shape[2:], jnp.float32)
    for offset in range(4):
        folded = folded + jnp.pad(pieces[:, offset], ((offset, 3 - offset), (0, 0), (0, 0), (0, 0)))
    return (mixed_out, grad_query, folded)

def reference(frame_in, token_ids, durations, valid_len, t_bin, token_table, enc_weight, mod_table, w_query, w_key, w_value, attn_grad):
    weights_all = jnp.concatenate([w_query, w_key, w_value], axis=1)
    grad_scale = 1.0 / math.sqrt(RECS * FRAMES)
    n_blocks = FRAMES // BLK

    def one_record(record_items):
        frames, record_ids, record_dur, valid_end, t_index, grad_in = record_items
        token_emb = jnp.take(token_table, record_ids, axis=0)
        token_ends = jnp.cumsum(record_dur, axis=1).astype(jnp.int32)
        local_pos = jnp.arange(F_DEV, dtype=jnp.int32)
        owner_tok = lax.optimization_barrier(jnp.sum((token_ends[:, None, :] <= local_pos[None, :, None]).astype(jnp.int32), axis=2)).astype(jnp.int32)
        frame_emb = jax.vmap(lambda table_rows, picks: jnp.take(table_rows, picks, axis=0))(token_emb, owner_tok).reshape(FRAMES, ENC)
        hidden_in = frames.astype(jnp.float32) + jnp.dot(frame_emb, enc_weight, preferred_element_type=jnp.float32)
        root_ms = jnp.sqrt(lax.optimization_barrier(jnp.mean(hidden_in * hidden_in, axis=1, keepdims=True)) + 1e-06)
        normed = hidden_in / root_ms
        modulation = lax.dynamic_index_in_dim(mod_table, t_index, 0, keepdims=False)
        gain_part = 1.0 + modulation[:D]
        shift_part = modulation[D:]
        modulated = rounded(normed * gain_part + shift_part)
        projected = rounded(jnp.dot(modulated, weights_all, preferred_element_type=jnp.float32))
        queries = projected[:, :QW]
        keys_values = projected[:, QW:]
        extended = jnp.concatenate([jnp.zeros((2 * BLK, 2 * QW), jnp.bfloat16), keys_values, jnp.zeros((BLK, 2 * QW), jnp.bfloat16)], axis=0)
        ext_blocks = extended.reshape(n_blocks + 3, BLK, 2, HEADS, HD)
        all_pos = jnp.arange(FRAMES, dtype=jnp.int32)
        query_pos = all_pos.reshape(n_blocks, BLK)
        key_pos = (jnp.arange(n_blocks, dtype=jnp.int32)[:, None] - 2) * BLK + jnp.arange(4 * BLK, dtype=jnp.int32)[None, :]
        grad_live = jnp.where((all_pos < valid_end)[:, None], grad_in, jnp.zeros_like(grad_in))
        attn_blocks, query_grad, ext_grad = attend_window(queries.reshape(n_blocks, BLK, HEADS, HD), ext_blocks[:, :, 0], ext_blocks[:, :, 1], grad_live.reshape(n_blocks, BLK, HEADS, HD), query_pos, key_pos, valid_end, FRAMES)
        ext_rows = ext_grad.reshape((n_blocks + 3) * BLK, 2 * QW)
        own_rows = rounded(ext_rows[2 * BLK:2 * BLK + FRAMES])
        grad_cat = jnp.concatenate([query_grad.reshape(FRAMES, QW), own_rows], axis=1)
        slab_rows = modulated.reshape(N_SEQ, F_DEV, D).astype(jnp.float32)
        slab_grads = grad_cat.reshape(N_SEQ, F_DEV, 3 * QW).astype(jnp.float32)
        slab_terms = jnp.einsum('sfd,sfc->sdc', slab_rows, slab_grads) * grad_scale
        record_sum = lax.optimization_barrier(jnp.sum(rounded(slab_terms).astype(jnp.float32), axis=0))
        hidden_grad = lax.dot_general(grad_cat, weights_all, (((1,), (1,)), ((), ())), preferred_element_type=jnp.float32)
        scaled_grad = hidden_grad * gain_part
        frame_grad = (scaled_grad - normed * lax.optimization_barrier(jnp.mean(scaled_grad * normed, axis=1, keepdims=True))) / root_ms
        return (attn_blocks.reshape(FRAMES, QW), frame_grad.astype(jnp.bfloat16), record_sum)
    attn_out, frame_grad, record_sums = lax.map(one_record, (frame_in, token_ids, durations, valid_len, t_bin, attn_grad))
    weight_grad = lax.optimization_barrier(jnp.sum(record_sums, axis=0))
    return (attn_out, frame_grad, weight_grad[:, :QW], weight_grad[:, QW:2 * QW], weight_grad[:, 2 * QW:])
```

```python
import functools
import math

import jax
import jax.numpy as jnp
from jax import lax
from jax.experimental import pallas as pl
from jax.experimental.pallas import tpu as pltpu
from jax.sharding import PartitionSpec as P

D = 1024
HEADS = 8
HD = 64
BLK = 48
QW = 512
GROUP = 4
GW = QW // GROUP
BF16 = jnp.bfloat16
F32 = jnp.float32


def partner(block, axis, bit):
    route = [(i, i ^ bit) for i in range(lax.axis_size(axis))]
    return lax.ppermute(block, axis, route)


def moved(block, axis, distance):
    devices = range(lax.axis_size(axis))
    route = [(i, i + distance) for i in devices if i + distance in devices]
    return lax.ppermute(block, axis, route)


def call(body, outs, scratch=(), cost=(1 << 28, 1 << 22), name=None):
    def run(info, *arrays):
        return pl.pallas_call(
            body,
            out_shape=[jax.ShapeDtypeStruct(shape, dtype) for shape, dtype in outs],
            in_specs=[pl.BlockSpec(memory_space=pltpu.SMEM)]
            + [pl.BlockSpec(memory_space=pltpu.VMEM)] * len(arrays),
            out_specs=[pl.BlockSpec(memory_space=pltpu.VMEM)] * len(outs),
            scratch_shapes=list(scratch),
            cost_estimate=pl.CostEstimate(
                flops=cost[0], bytes_accessed=cost[1], transcendentals=0
            ),
            name=name,
        )(info, *arrays)

    return run


def embed_body(
    table_bits,
    table_rows,
    info,
    keep,
    other,
    table_a,
    table_b,
    enc,
    mod_row,
    modulated,
    hidden_own,
    grad_all,
    table,
):
    half = table_a.shape[0]
    n_frames = hidden_own.shape[0]
    table[:half] = table_a[...]
    table[half:] = table_b[...]
    gain = 1.0 + mod_row[:, :D]
    shift = mod_row[:, D:]
    for k in range(GROUP):
        src = keep if k % 2 == 0 else other
        rows = pl.ds((k // 2) * n_frames, n_frames)
        slab = jnp.bitwise_xor(info[1], k)
        dest = pl.ds(pl.multiple_of(slab * n_frames, n_frames), n_frames)
        marks = src[rows, D + GW :].astype(F32)
        away = jnp.bitwise_xor(marks[:, 0:1].astype(jnp.int32), info[0])
        place = marks[:, 1:2].astype(jnp.int32)
        for j, bit in enumerate(table_bits):
            place = place + jnp.where((away & bit) != 0, (1 << j) * table_rows, 0)
        spots = lax.broadcasted_iota(jnp.int32, (n_frames, 2 * half), 1)
        chosen = jnp.where(spots == place, 1.0, 0.0).astype(BF16)
        emb = jnp.dot(chosen, table[...], preferred_element_type=F32).astype(BF16)
        hidden = src[rows, :D].astype(F32) + jnp.dot(
            emb, enc[...], preferred_element_type=F32
        )
        root_ms = jnp.sqrt(jnp.mean(hidden * hidden, axis=1, keepdims=True) + 1e-06)
        normed = hidden * (1.0 / root_ms)
        modulated[dest, :] = (normed * gain + shift).astype(BF16)
        grad_all[dest, :] = src[rows, D : D + GW]
        if k == 0:
            hidden_own[...] = hidden


def project_body(offs, info, modulated, w_a, w_b, qkv, weights, kv_tail, kv_head):
    n_rows = w_a.shape[0] * 2 // len(offs)
    for j, off in enumerate(offs):
        src = w_a if j < len(offs) // 2 else w_b
        row = (j % (len(offs) // 2)) * n_rows
        dest = pl.multiple_of(jnp.bitwise_xor(info[0], off) * n_rows, n_rows)
        weights[pl.ds(dest, n_rows), :] = src[pl.ds(row, n_rows), :]
    out = jnp.dot(modulated[...], weights[...], preferred_element_type=F32).astype(BF16)
    qkv[...] = out
    kv_tail[...] = out[out.shape[0] - 2 * BLK :, GW:]
    kv_head[...] = out[:BLK, GW:]


def attend_body(
    info,
    qkv,
    before,
    after,
    grad_all,
    mixed,
    query_grad,
    kv_grad,
    to_prev,
    to_next,
    k_ext,
    v_ext,
    kv_ext,
):
    total = qkv.shape[0]
    n_frames = total // GROUP
    span = k_ext.shape[0] - total + n_frames
    for ext, lane in ((k_ext, 0), (v_ext, GW)):
        ext[: 2 * BLK] = before[:, lane : lane + GW]
        ext[2 * BLK : 2 * BLK + total] = qkv[:, GW + lane : 2 * GW + lane]
        ext[2 * BLK + total : 3 * BLK + total] = after[:, lane : lane + GW]
        ext[3 * BLK + total :] = jnp.zeros((ext.shape[0] - 3 * BLK - total, GW), BF16)
    kv_ext[...] = jnp.zeros_like(kv_ext)
    base = info[2]
    valid_end = info[3]
    frames_total = info[4]
    q_row = lax.broadcasted_iota(jnp.int32, (n_frames, span), 0)
    k_col = lax.broadcasted_iota(jnp.int32, (n_frames, span), 1)
    q_edge = jnp.zeros_like(q_row)
    for edge in range(BLK, n_frames, BLK):
        q_edge = jnp.where(q_row >= edge, edge, q_edge)
    banded = (k_col >= q_edge) & (k_col < q_edge + 4 * BLK)
    lanes = lax.broadcasted_iota(jnp.int32, (n_frames, GW), 1)
    row_ids = lax.broadcasted_iota(jnp.int32, (n_frames, GW), 0)
    inv_scale = 1.0 / math.sqrt(HD)
    for sl in range(GROUP):
        start = base + sl * n_frames
        rows = pl.ds(sl * n_frames, n_frames)
        window = pl.ds(sl * n_frames, span)
        k_pos = k_col + (start - 2 * BLK)
        allowed = (
            banded
            & (k_pos >= 0)
            & (k_pos < frames_total)
            & ((k_pos < valid_end) | (q_row + start >= valid_end))
        )
        queries = qkv[rows, :GW]
        grads = grad_all[rows, :]
        grads = jnp.where(row_ids + start < valid_end, grads, jnp.zeros_like(grads))
        keys = k_ext[window, :]
        values = v_ext[window, :]
        mixed_sum = jnp.zeros((n_frames, GW), F32)
        query_sum = jnp.zeros((n_frames, GW), F32)
        for h in range(GW // HD):
            mine = (lanes >= h * HD) & (lanes < (h + 1) * HD)
            q_h = jnp.where(mine, queries, jnp.zeros_like(queries))
            g_h = jnp.where(mine, grads, jnp.zeros_like(grads))
            scores = (
                lax.dot_general(
                    q_h, keys, (((1,), (1,)), ((), ())), preferred_element_type=F32
                )
                * inv_scale
            )
            scores = jnp.where(allowed, scores, -1e30)
            top = jnp.max(scores, axis=-1, keepdims=True)
            weights = jnp.where(allowed, jnp.exp(scores - top), 0.0)
            prob = weights * (1.0 / jnp.sum(weights, axis=-1, keepdims=True))
            prob_low = prob.astype(BF16)
            grad_prob = lax.dot_general(
                g_h, values, (((1,), (1,)), ((), ())), preferred_element_type=F32
            )
            centre = jnp.sum(prob * grad_prob, axis=-1, keepdims=True)
            grad_score = (prob * (grad_prob - centre) * inv_scale).astype(BF16)
            mixed_h = jnp.dot(prob_low, values, preferred_element_type=F32)
            mixed_sum = jnp.where(mine, mixed_h, mixed_sum)
            query_h = jnp.dot(grad_score, keys, preferred_element_type=F32)
            query_sum = jnp.where(mine, query_h, query_sum)
            kv_ext[window, :GW] += lax.dot_general(
                grad_score, q_h, (((0,), (0,)), ((), ())), preferred_element_type=F32
            )
            kv_ext[window, GW:] += lax.dot_general(
                prob_low, g_h, (((0,), (0,)), ((), ())), preferred_element_type=F32
            )
        mixed[rows, :] = mixed_sum.astype(BF16)
        query_grad[rows, :] = query_sum.astype(BF16)
    kv_grad[...] = kv_ext[2 * BLK : 2 * BLK + total, :]
    to_prev[...] = kv_ext[: 2 * BLK, :]
    to_next[...] = kv_ext[2 * BLK + total : 3 * BLK + total, :]


def reduce_body(
    grad_scale,
    info,
    modulated,
    weights,
    mixed,
    query_grad,
    kv_grad,
    from_next,
    from_prev,
    send_back,
    keep_back,
    *rest,
):
    *terms, grad_cat = rest
    total = modulated.shape[0]
    n_frames = total // GROUP
    tail = total - 2 * BLK
    grad_cat[:, :GW] = query_grad[...]
    grad_cat[:BLK, GW:] = (kv_grad[:BLK] + from_prev[...]).astype(BF16)
    grad_cat[BLK:tail, GW:] = kv_grad[BLK:tail].astype(BF16)
    grad_cat[tail:, GW:] = (kv_grad[tail:] + from_next[...]).astype(BF16)
    width = D // len(terms)
    for k, term in enumerate(terms):
        cols = pl.multiple_of(jnp.bitwise_xor(info[5], k) * width, width)
        term[...] = (
            lax.dot_general(
                modulated[:, pl.ds(cols, width)],
                grad_cat[...],
                (((0,), (0,)), ((), ())),
                preferred_element_type=F32,
            )
            * grad_scale
        ).astype(BF16)
    for k in range(GROUP):
        dest = keep_back if k % 2 == 0 else send_back
        rows = pl.ds((k // 2) * n_frames, n_frames)
        slab = jnp.bitwise_xor(info[1], k)
        src = pl.ds(pl.multiple_of(slab * n_frames, n_frames), n_frames)
        dest[rows, :D] = lax.dot_general(
            grad_cat[src, :], weights[...], (((1,), (1,)), ((), ())), preferred_element_type=F32
        ).astype(BF16)
        dest[rows, D:] = mixed[src, :]


def frame_body(info, hidden_own, mod_row, keep, near, far, frame_grad, attn_out):
    n_frames = hidden_own.shape[0]
    hidden = hidden_own[...]
    root_ms = jnp.sqrt(jnp.mean(hidden * hidden, axis=1, keepdims=True) + 1e-06)
    inv_root = 1.0 / root_ms
    normed = hidden * inv_root
    hidden_grad = (
        keep[:n_frames, :D].astype(F32)
        + near[:n_frames, :D].astype(F32)
        + far[:, :D].astype(F32)
    )
    scaled = hidden_grad * (1.0 + mod_row[:, :D])
    frame_grad[...] = (
        (scaled - normed * jnp.mean(scaled * normed, axis=1, keepdims=True)) * inv_root
    ).astype(BF16)
    for k, part in (
        (0, keep[:n_frames, D:]),
        (1, near[:n_frames, D:]),
        (2, far[:, D : D + GW]),
        (3, far[:, D + GW :]),
    ):
        cols = pl.multiple_of(jnp.bitwise_xor(info[1], k) * GW, GW)
        attn_out[:, pl.ds(cols, GW)] = part


def spread_body(info, own, got, query_out, key_out, value_out):
    for k, (src, lane) in enumerate(
        ((own, 0), (got, 0), (own, 3 * GW), (got, 3 * GW))
    ):
        cols = pl.multiple_of(jnp.bitwise_xor(info[1], k) * GW, GW)
        for j, out in enumerate((query_out, key_out, value_out)):
            part = src[:, lane + j * GW : lane + (j + 1) * GW]
            out[:, pl.ds(cols, GW)] = part.astype(F32)


def shards(
    frame_in,
    token_ids,
    durations,
    valid_len,
    t_bin,
    token_table,
    enc_weight,
    mod_table,
    w_query,
    w_key,
    w_value,
    attn_grad,
):
    frames = frame_in[0]
    n_frames = frames.shape[0]
    seq_count = lax.axis_size("seq")
    dp_count = lax.axis_size("dp")
    seq_index = lax.axis_index("seq")
    lines = seq_count // GROUP
    line_bits = [GROUP << j for j in reversed(range(lines.bit_length() - 1))]
    table_rows = token_table.shape[0]
    w_rows = w_query.shape[0]
    total = GROUP * n_frames
    member = seq_index % GROUP
    line = seq_index // GROUP
    low = seq_index % 2 == 0
    high = member < 2
    info = jnp.stack(
        [
            seq_index,
            member,
            line * total,
            valid_len[0],
            jnp.int32(n_frames * seq_count),
            line,
        ]
    ).astype(jnp.int32)

    table = token_table
    table_bits = line_bits + [2]
    for bit in table_bits:
        table = jnp.concatenate([table, partner(table, "seq", bit)], axis=0)
    table_b = partner(table, "seq", 1)
    table_bits = table_bits + [1]

    w_cat = jnp.concatenate(
        [
            w[:, m * GW : (m + 1) * GW]
            for m in range(GROUP)
            for w in (w_query, w_key, w_value)
        ],
        axis=1,
    )
    half = 6 * GW
    w_got = partner(jnp.where(high, w_cat[:, half:], w_cat[:, :half]), "seq", 2)
    w_pair = jnp.concatenate(
        [jnp.where(high, w_cat[:, :half], w_cat[:, half:]), w_got], axis=0
    )
    half = 3 * GW
    w_got = partner(jnp.where(low, w_pair[:, half:], w_pair[:, :half]), "seq", 1)
    w_own = jnp.concatenate(
        [jnp.where(low, w_pair[:, :half], w_pair[:, half:]), w_got], axis=0
    )
    offs = [0, 2, 1, 3]
    for bit in line_bits[:-1]:
        w_own = jnp.concatenate([w_own, partner(w_own, "seq", bit)], axis=0)
        offs = offs + [off ^ bit for off in offs]
    w_far = partner(w_own, "seq", line_bits[-1])
    offs = offs + [off ^ line_bits[-1] for off in offs]

    lengths = durations[0, 0]
    n_tok = lengths.shape[0]
    order = jnp.arange(n_tok, dtype=jnp.int32)
    ends = jnp.sum(jnp.where(order[:, None] <= order[None, :], lengths[:, None], 0), axis=0)
    local_pos = jnp.arange(n_frames, dtype=jnp.int32)[:, None]
    held = (local_pos < ends[None, :]) & (local_pos >= (ends - lengths)[None, :])
    wanted = jnp.sum(jnp.where(held, token_ids[0], 0), axis=1, keepdims=True)
    lane = jnp.arange(GW, dtype=jnp.int32)[None, :]
    marks = jnp.where(
        lane == 0,
        wanted // table_rows,
        jnp.where(lane == 1, wanted % table_rows, 0),
    ).astype(BF16)
    grads = attn_grad[0]
    g_here = jnp.where(high, grads[:, : 2 * GW], grads[:, 2 * GW :])
    g_there = jnp.where(high, grads[:, 2 * GW :], grads[:, : 2 * GW])
    got = partner(jnp.concatenate([frames, g_there, marks], axis=1), "seq", 2)
    pair = jnp.concatenate(
        [jnp.concatenate([frames, g_here, marks], axis=1), got], axis=0
    )
    g_low, g_high = pair[:, D : D + GW], pair[:, D + GW : D + 2 * GW]
    keep = jnp.concatenate(
        [pair[:, :D], jnp.where(low, g_low, g_high), pair[:, D + 2 * GW :]], axis=1
    )
    give = jnp.concatenate(
        [pair[:, :D], jnp.where(low, g_high, g_low), pair[:, D + 2 * GW :]], axis=1
    )
    other = partner(give, "seq", 1)

    mod_row = lax.dynamic_slice_in_dim(mod_table, t_bin[0], 1, 0)
    modulated, hidden_own, grad_all = call(
        functools.partial(embed_body, table_bits, table_rows),
        [((total, D), BF16), ((n_frames, D), F32), ((total, GW), BF16)],
        [pltpu.VMEM((2 * table.shape[0], table.shape[1]), BF16)],
        cost=(2 << 30, 6 << 20),
        name="embed",
    )(info, keep, other, table, table_b, enc_weight, mod_row)
    qkv, weights, kv_tail, kv_head = call(
        functools.partial(project_body, offs),
        [
            ((total, 3 * GW), BF16),
            ((D, 3 * GW), BF16),
            ((2 * BLK, 2 * GW), BF16),
            ((BLK, 2 * GW), BF16),
        ],
        cost=(1 << 29, 3 << 20),
        name="project",
    )(info, modulated, w_own, w_far)
    before = moved(kv_tail, "seq", GROUP)
    after = moved(kv_head, "seq", -GROUP)
    span = -(-(n_frames + 3 * BLK) // 128) * 128
    ext_rows = total - n_frames + span
    mixed, query_grad, kv_grad, to_prev, to_next = call(
        attend_body,
        [
            ((total, GW), BF16),
            ((total, GW), BF16),
            ((total, 2 * GW), F32),
            ((2 * BLK, 2 * GW), F32),
            ((BLK, 2 * GW), F32),
        ],
        [
            pltpu.VMEM((ext_rows, GW), BF16),
            pltpu.VMEM((ext_rows, GW), BF16),
            pltpu.VMEM((ext_rows, 2 * GW), F32),
        ],
        cost=(1 << 30, 2 << 20),
        name="attend",
    )(info, qkv, before, after, grad_all)
    from_next = moved(to_prev, "seq", -GROUP)
    from_prev = moved(to_next, "seq", GROUP)
    grad_scale = 1.0 / math.sqrt(dp_count * n_frames * seq_count)
    send_back, keep_back, *terms = call(
        functools.partial(reduce_body, grad_scale),
        [((2 * n_frames, D + GW), BF16)] * 2 + [((D // lines, 3 * GW), BF16)] * lines,
        [pltpu.VMEM((total, 3 * GW), BF16)],
        cost=(1 << 30, 4 << 20),
        name="reduce",
    )(info, modulated, weights, mixed, query_grad, kv_grad, from_next, from_prev)

    acc = terms[0].astype(F32)
    for k in range(1, lines):
        acc = acc + partner(terms[k], "seq", GROUP * k).astype(F32)
    bit = 1
    while bit < dp_count:
        part = acc.astype(BF16)
        acc = part.astype(F32) + partner(part, "dp", bit).astype(F32)
        bit *= 2
    rows = acc.astype(BF16)
    cut = 2 * w_rows
    got = partner(jnp.where(high, rows[cut:], rows[:cut]), "seq", 2)
    pair = jnp.concatenate([jnp.where(high, rows[:cut], rows[cut:]), got], axis=1)
    w_give = jnp.where(low, pair[w_rows:], pair[:w_rows])
    w_keep = jnp.where(low, pair[:w_rows], pair[w_rows:])
    w_got = partner(w_give, "seq", 1)
    grad_q, grad_k, grad_v = call(
        spread_body, [((w_rows, QW), F32)] * 3, cost=(1 << 16, 1 << 19), name="spread"
    )(info, w_keep, w_got)

    near = partner(send_back, "seq", 1)
    far_sum = (
        keep_back[n_frames:, :D].astype(F32) + near[n_frames:, :D].astype(F32)
    ).astype(BF16)
    far = partner(
        jnp.concatenate([far_sum, keep_back[n_frames:, D:], near[n_frames:, D:]], axis=1),
        "seq",
        2,
    )
    frame_grad, attn_out = call(
        frame_body,
        [((n_frames, D), BF16), ((n_frames, QW), BF16)],
        cost=(1 << 24, 2 << 20),
        name="frame",
    )(info, hidden_own, mod_row, keep_back, near, far)
    return attn_out[None], frame_grad[None], grad_q, grad_k, grad_v


def solution(mesh):
    placed = (
        P("dp", "seq", None),
        P("dp", "seq", None),
        P("dp", "seq", None),
        P("dp"),
        P("dp"),
        P("seq", None),
        P(),
        P(),
        P("seq", None),
        P("seq", None),
        P("seq", None),
        P("dp", "seq", None),
    )
    return jax.shard_map(
        shards,
        mesh=mesh,
        in_specs=placed,
        out_specs=(
            P("dp", "seq", None),
            P("dp", "seq", None),
            P("seq", None),
            P("seq", None),
            P("seq", None),
        ),
        check_vma=False,
    )
```
